256 devices in a mesh: rows: 8 (over x, core), vocab: 32 (over z, y).
Axes of the slice: x: 4, y: 4, z: 8, core: 2. Of those that a mesh axis runs over, the one named last changes fastest.
Arguments:
- draft_hidden: bfloat16 [4096, 2048], P('rows'), may hold values from -128 to 128
- teacher_hidden: bfloat16 [4096, 8192], P('rows'), may hold values from -128 to 128
- draft_head: bfloat16 [2048, 32768], P(None, 'vocab'), may hold values from -4 to 4
- teacher_head: bfloat16 [8192, 32768], P(None, ('vocab', 'rows')), may hold values from -4 to 4
- row_weight: float32 [4096], P('rows'), may hold values from 1 to 16
Outputs:
- grad_hidden: bfloat16 [4096, 2048], P('rows')
- grad_head: bfloat16 [2048, 32768], P('rows', 'vocab')
- kl_rows: float32 [4096], P('rows')
The draws below stay inside these ranges and needn't reach their ends.
All inputs are finite; a program needn't handle non-finite values.
Results may differ from the reference program's by a relative error of at most 0.0051.
Values may be sent and summed in bfloat16 or wider, within the bound.
No kernel may reach another device: no remote copies, remote signals or barrier semaphores. Data moves between devices by JAX's collectives and lax.ppermute only.
A program may use at most 192 MiB of HBM per device.

```python
import math
import jax
import jax.numpy as jnp

D_DRAFT = 2048
D_TEACH = 8192
TOKENS = 4096
VOCAB = 32768


def make_pair(key, salt, width, spread):
    folded = jax.random.fold_in(key, salt)
    key_weight, key_state = jax.random.split(folded, 2)
    weight = spread * jnp.clip(jax.random.normal(key_weight, (width, VOCAB), jnp.float32), -6.0, 6.0)
    states = jnp.clip(jax.random.normal(key_state, (TOKENS, width), jnp.float32), -6.0, 6.0)
    return (weight, states)


def draw_draft_hidden(key, part):
    return make_pair(key, 11, D_DRAFT, 3.5 / D_DRAFT ** 0.5)[1].astype(jnp.bfloat16)


def draw_draft_head(key, part):
    return make_pair(key, 11, D_DRAFT, 3.5 / D_DRAFT ** 0.5)[0].astype(jnp.bfloat16)


def draw_teacher_hidden(key, part):
    return make_pair(key, 23, D_TEACH, 4.0 / D_TEACH ** 0.5)[1].astype(jnp.bfloat16)


def draw_teacher_head(key, part):
    return make_pair(key, 23, D_TEACH, 4.0 / D_TEACH ** 0.5)[0].astype(jnp.bfloat16)


def steps_of(own_key, shape, cuts, low, top_value):
    loudness = 1.0
    for dim, blocks in cuts:
        draws = jax.random.uniform(jax.random.fold_in(jax.random.fold_in(own_key, 6), dim), (blocks,), jnp.float32, low / len(cuts), top_value / len(cuts))
        loudness = loudness * jnp.repeat(jnp.exp(draws), shape[dim] // blocks).reshape((-1,) + (1,) * (len(shape) - 1 - dim))
    return loudness


def setup_inputs(seed: int = 0) -> dict:
    key_list = jax.random.split(jax.random.key(seed), 6)
    draft_hidden = draw_draft_hidden(jax.random.fold_in(key_list[5], 71), 0)
    teacher_hidden = draw_teacher_hidden(jax.random.fold_in(key_list[5], 71), 0)
    draft_head = draw_draft_head(jax.random.fold_in(key_list[5], 71), 0)
    teacher_head = draw_teacher_head(jax.random.fold_in(key_list[5], 71), 0)
    row_weight = jnp.clip(jnp.exp(math.log(16.0) - 2.7725887 * jax.random.uniform(key_list[4], (TOKENS,), jnp.float32) ** steps_of(key_list[4], (TOKENS,), ((0, 8),), -0.2, 0.2)), 1.0, 16.0)
    return {"draft_hidden": draft_hidden, "teacher_hidden": teacher_hidden, "draft_head": draft_head, "teacher_head": teacher_head, "row_weight": row_weight}


def log_total(logits):
    peak = jnp.max(logits, axis=1)
    return peak + jnp.log(jnp.sum(jnp.exp(logits - peak[:, None]), axis=1))


def reference(draft_hidden, teacher_hidden, draft_head, teacher_head, row_weight):
    draft_logits = jnp.dot(draft_hidden, draft_head, preferred_element_type=jnp.float32)
    teacher_logits = jnp.dot(teacher_hidden, teacher_head, preferred_element_type=jnp.float32)
    draft_lse = log_total(draft_logits)
    teacher_lse = log_total(teacher_logits)
    teacher_prob = jnp.exp(teacher_logits - teacher_lse[:, None])
    draft_prob = jnp.exp(draft_logits - draft_lse[:, None])
    kl_rows = row_weight * (jnp.sum(teacher_prob * (teacher_logits - draft_logits), axis=1) - teacher_lse + draft_lse)
    grad_logits = (row_weight[:, None] * (draft_prob - teacher_prob)).astype(jnp.bfloat16)
    grad_hidden = jnp.dot(grad_logits, draft_head.T, preferred_element_type=jnp.float32).astype(jnp.bfloat16)
    grad_head = jnp.dot(draft_hidden.T, grad_logits, preferred_element_type=jnp.float32).astype(jnp.bfloat16)
    return grad_hidden, grad_head, kl_rows
```

```python
import jax
import jax.numpy as jnp
from jax import lax
from jax.sharding import Mesh
from jax.sharding import PartitionSpec as P


ROWS = ("x", "core")
VOCAB = ("z", "y")
VOCAB_ROWS = ("z", "y", "x", "core")


def shifted(x, axis, by):
    n = lax.axis_size(axis)
    return lax.ppermute(x, axis, [(i, (i + by) % n) for i in range(n)])


def dot(a, b, contract):
    return lax.dot_general(a, b, (contract, ((), ())), preferred_element_type=jnp.float32)


def exchanged(pieces, axis):
    return lax.all_to_all(pieces, axis, 0, 0, tiled=True)


def sent_to_all(x, axis):
    return exchanged(jnp.broadcast_to(x[None], (lax.axis_size(axis), *x.shape)), axis)


def combined(pieces):
    draft_top = jnp.max(pieces[:, 0], axis=0)
    teach_top = jnp.max(pieces[:, 2], axis=0)
    draft_scale = jnp.exp(pieces[:, 0] - draft_top)
    teach_scale = jnp.exp(pieces[:, 2] - teach_top)
    return jnp.stack(
        [
            draft_top,
            jnp.sum(pieces[:, 1] * draft_scale, axis=0),
            teach_top,
            jnp.sum(pieces[:, 3] * teach_scale, axis=0),
            jnp.sum(pieces[:, 4] * teach_scale, axis=0),
        ]
    )


def teacher_product(hidden, own):
    place, core = lax.axis_index("x"), lax.axis_index("core")
    ring = lax.axis_size("x")
    half = own.shape[0] // 2
    behind = shifted(own, "x", 1)
    ahead = shifted(own, "x", -1)
    far_top = shifted(behind[:half], "x", 1)
    far_low = shifted(ahead[half:], "x", -1)

    def product(states, piece):
        other = shifted(piece, "core", 1)
        pair = jnp.where(
            core == 0,
            jnp.concatenate([piece, other], axis=1),
            jnp.concatenate([other, piece], axis=1),
        )
        return dot(states, pair, ((1,), (0,)))

    behind, ahead = product(hidden, behind), product(hidden, ahead)
    own_part = product(hidden, own)
    far = product(hidden[:, :half], far_top) + product(hidden[:, half:], far_low)
    width = 2 * own.shape[1]
    logits = jnp.zeros((hidden.shape[0], ring * width), jnp.float32)
    for step, part in (
        (0, own_part),
        (-1, behind),
        (1, ahead),
        (2, far),
    ):
        at = (place + step) % ring
        logits = lax.dynamic_update_slice(logits, part, (0, at * width))
    return logits


def swapped(pieces, axis):
    n, place = lax.axis_size(axis), lax.axis_index(axis)
    found = []
    for by in range(n):
        piece = lax.dynamic_index_in_dim(pieces, (place + by) % n, 0, keepdims=False)
        found.append(shifted(piece, axis, by) if by else piece)
    return found


def gathered(block, axis):
    n, place = lax.axis_size(axis), lax.axis_index(axis)
    whole = jnp.zeros((n, *block.shape), block.dtype)
    for by in range(n):
        piece = shifted(block, axis, by) if by else block
        whole = lax.dynamic_update_index_in_dim(whole, piece, (place - by) % n, 0)
    return whole


def added(pieces):
    return sum(piece.astype(jnp.float32) for piece in pieces).astype(jnp.bfloat16)


def summed_head(draft_hidden, grad_logits):
    core = lax.axis_index("core")
    tokens, width = draft_hidden.shape
    ring = lax.axis_size("x")
    strips = draft_hidden.reshape(tokens, ring, 2, width // (2 * ring))

    def strip(which):
        return lax.dynamic_index_in_dim(strips, which, 2, keepdims=False).reshape(tokens, width // 2)

    away = dot(strip(1 - core), grad_logits, ((0,), (0,))).astype(jnp.bfloat16)
    away = shifted(away, "core", 1)
    mine = dot(strip(core), grad_logits, ((0,), (0,)))
    pair = (mine + away.astype(jnp.float32)).astype(jnp.bfloat16)
    pieces = swapped(pair.reshape(ring, -1, pair.shape[1]), "x")
    return added(pieces)


def columns_apart(x, n):
    return jnp.moveaxis(x.reshape(x.shape[0], n, -1), 1, 0)


def columns_together(x):
    return jnp.moveaxis(x, 0, 1).reshape(x.shape[1], -1)


def summed(part):
    n, m = lax.axis_size("y"), lax.axis_size("z")
    cut = part.shape[0] * 3 // 4
    most, rest = part[:cut], part[cut:]
    most = swapped(most.reshape(n, -1, part.shape[1]), "y")
    rest = exchanged(rest.reshape(m, -1, part.shape[1]), "z")
    most, rest = lax.optimization_barrier((most, rest))
    most, rest = columns_apart(added(most), m), columns_apart(added(rest), n)
    most = exchanged(most, "z")
    rest = swapped(rest, "y")
    most, rest = lax.optimization_barrier((most, rest))
    most, rest = added(most), added(rest)
    most = sent_to_all(most, "z")
    rest = gathered(rest, "y")
    most, rest = lax.optimization_barrier((most, rest))
    most, rest = columns_together(most), columns_together(rest)
    most = gathered(most, "y")
    rest = sent_to_all(rest, "z")
    return jnp.concatenate([most.reshape(cut, -1), rest.reshape(part.shape[0] - cut, -1)])


def stage(draft_hidden, teacher_hidden, draft_head, teacher_head, row_weight):
    draft_logits = dot(draft_hidden, draft_head, ((1,), (0,)))
    teacher_logits = teacher_product(teacher_hidden, teacher_head)
    local_draft = jnp.max(draft_logits, axis=1)
    local_teach = jnp.max(teacher_logits, axis=1)
    teach_exp = jnp.exp(teacher_logits - local_teach[:, None])
    stats = jnp.stack(
        [
            local_draft,
            jnp.sum(jnp.exp(draft_logits - local_draft[:, None]), axis=1),
            local_teach,
            jnp.sum(teach_exp, axis=1),
            jnp.sum(teach_exp * (teacher_logits - draft_logits), axis=1),
        ]
    )
    stats = combined(sent_to_all(stats, "y"))
    draft_top, draft_sum, teach_top, teach_sum, teach_gap = combined(sent_to_all(stats, "z"))
    draft_lse = draft_top + jnp.log(draft_sum)
    teacher_lse = teach_top + jnp.log(teach_sum)
    kl_rows = row_weight * (teach_gap / teach_sum - teacher_lse + draft_lse)
    teacher_prob = jnp.exp(teacher_logits - teacher_lse[:, None])
    draft_prob = jnp.exp(draft_logits - draft_lse[:, None])
    grad_logits = (row_weight[:, None] * (draft_prob - teacher_prob)).astype(jnp.bfloat16)
    grad_head = summed_head(draft_hidden, grad_logits)
    hidden_part = dot(grad_logits, draft_head, ((1,), (1,))).astype(jnp.bfloat16)
    grad_hidden = summed(hidden_part)
    return (grad_hidden, grad_head, kl_rows)


def solution(mesh):
    finer = Mesh(mesh.devices.reshape(4, 2, 8, 4), ("x", "core", "z", "y"))
    return jax.shard_map(
        stage,
        mesh=finer,
        in_specs=(P(ROWS, None), P(ROWS, None), P(None, VOCAB), P(None, VOCAB_ROWS), P(ROWS)),
        out_specs=(P(ROWS, None), P(ROWS, VOCAB), P(ROWS)),
        check_vma=False,
    )
```

```python
import jax
import jax.numpy as jnp
from jax import lax
from jax.sharding import Mesh
from jax.sharding import PartitionSpec as P


ROWS = ("x", "core")
VOCAB = ("z", "y")
VOCAB_ROWS = ("z", "y", "x", "core")


def shifted(x, axis, by):
    n = lax.axis_size(axis)
    return lax.ppermute(x, axis, [(i, (i + by) % n) for i in range(n)])


def dot(a, b, contract):
    return lax.dot_general(a, b, (contract, ((), ())), preferred_element_type=jnp.float32)


def exchanged(pieces, axis):
    return lax.all_to_all(pieces, axis, 0, 0, tiled=True)


def sent_to_all(x, axis):
    return exchanged(jnp.broadcast_to(x[None], (lax.axis_size(axis), *x.shape)), axis)


def combined(pieces):
    draft_top = jnp.max(pieces[:, 0], axis=0)
    teach_top = jnp.max(pieces[:, 2], axis=0)
    draft_scale = jnp.exp(pieces[:, 0] - draft_top)
    teach_scale = jnp.exp(pieces[:, 2] - teach_top)
    return jnp.stack(
        [
            draft_top,
            jnp.sum(pieces[:, 1] * draft_scale, axis=0),
            teach_top,
            jnp.sum(pieces[:, 3] * teach_scale, axis=0),
            jnp.sum(pieces[:, 4] * teach_scale, axis=0),
        ]
    )


def teacher_product(hidden, own):
    place, core = lax.axis_index("x"), lax.axis_index("core")
    ring = lax.axis_size("x")

    def turned(piece, way):
        pairs = [
            (2 * i + c, 2 * ((i + (way if c == 0 else -way)) % ring) + c)
            for i in range(ring)
            for c in range(2)
        ]
        return lax.ppermute(piece, ROWS, pairs)

    def product(mine, others):
        pair = jnp.where(
            core == 0,
            jnp.concatenate([mine, others], axis=1),
            jnp.concatenate([others, mine], axis=1),
        )
        return dot(hidden, pair, ((1,), (0,)))

    behind, ahead = turned(own, 1), turned(own, -1)
    far = turned(behind, 1)
    own_part = product(own, shifted(own, "core", 1))
    behind_part = product(behind, shifted(ahead, "core", 1))
    ahead_part = product(ahead, shifted(behind, "core", 1))
    far_part = product(far, shifted(far, "core", 1))
    width = 2 * own.shape[1]
    back = jnp.where(core == 0, ring - 1, 1)
    logits = jnp.zeros((hidden.shape[0], ring * width), jnp.float32)
    for step, part in ((0, own_part), (back, behind_part), (ring - back, ahead_part), (2, far_part)):
        at = (place + step) % ring
        logits = lax.dynamic_update_slice(logits, part, (0, at * width))
    return logits


def swapped(pieces, axis):
    n, place = lax.axis_size(axis), lax.axis_index(axis)
    found = []
    for by in range(n):
        piece = lax.dynamic_index_in_dim(pieces, (place + by) % n, 0, keepdims=False)
        found.append(shifted(piece, axis, by) if by else piece)
    return found


def gathered(block, axis):
    n, place = lax.axis_size(axis), lax.axis_index(axis)
    whole = jnp.zeros((n, *block.shape), block.dtype)
    for by in range(n):
        piece = shifted(block, axis, by) if by else block
        whole = lax.dynamic_update_index_in_dim(whole, piece, (place - by) % n, 0)
    return whole


def added(pieces):
    return sum(piece.astype(jnp.float32) for piece in pieces).astype(jnp.bfloat16)


def summed_head(draft_hidden, grad_logits):
    core = lax.axis_index("core")
    tokens, width = draft_hidden.shape
    ring = lax.axis_size("x")
    strips = draft_hidden.reshape(tokens, ring, 2, width // (2 * ring))

    def strip(which):
        return lax.dynamic_index_in_dim(strips, which, 2, keepdims=False).reshape(tokens, width // 2)

    away = dot(strip(1 - core), grad_logits, ((0,), (0,))).astype(jnp.bfloat16)
    away = shifted(away, "core", 1)
    mine = dot(strip(core), grad_logits, ((0,), (0,)))
    pair = (mine + away.astype(jnp.float32)).astype(jnp.bfloat16)
    pieces = swapped(pair.reshape(ring, -1, pair.shape[1]), "x")
    return added(pieces)


def summed(part):
    n, m = lax.axis_size("y"), lax.axis_size("z")
    pieces = swapped(part.reshape(n, -1, part.shape[1]), "y")
    rows = added(pieces)
    pieces = exchanged(rows.reshape(m, -1, rows.shape[1]), "z")
    block = added(pieces)
    rows = sent_to_all(block, "z").reshape(rows.shape)
    return gathered(rows, "y").reshape(part.shape)


def stage(draft_hidden, teacher_hidden, draft_head, teacher_head, row_weight):
    draft_logits = dot(draft_hidden, draft_head, ((1,), (0,)))
    local_draft = jnp.max(draft_logits, axis=1)
    teacher_logits = teacher_product(teacher_hidden, teacher_head)
    local_teach = jnp.max(teacher_logits, axis=1)
    teach_exp = jnp.exp(teacher_logits - local_teach[:, None])
    stats = jnp.stack(
        [
            local_draft,
            jnp.sum(jnp.exp(draft_logits - local_draft[:, None]), axis=1),
            local_teach,
            jnp.sum(teach_exp, axis=1),
            jnp.sum(teach_exp * (teacher_logits - draft_logits), axis=1),
        ]
    )
    stats = combined(sent_to_all(stats, "y"))
    draft_top, draft_sum, teach_top, teach_sum, teach_gap = combined(sent_to_all(stats, "z"))
    draft_lse = draft_top + jnp.log(draft_sum)
    teacher_lse = teach_top + jnp.log(teach_sum)
    kl_rows = row_weight * (teach_gap / teach_sum - teacher_lse + draft_lse)
    teacher_prob = jnp.exp(teacher_logits - teacher_lse[:, None])
    draft_prob = jnp.exp(draft_logits - draft_lse[:, None])
    grad_logits = (row_weight[:, None] * (draft_prob - teacher_prob)).astype(jnp.bfloat16)
    grad_head = summed_head(draft_hidden, grad_logits)
    hidden_part = dot(grad_logits, draft_head, ((1,), (1,))).astype(jnp.bfloat16)
    grad_hidden = summed(hidden_part)
    return (grad_hidden, grad_head, kl_rows)


def solution(mesh):
    finer = Mesh(mesh.devices.reshape(4, 2, 8, 4), ("x", "core", "z", "y"))
    return jax.shard_map(
        stage,
        mesh=finer,
        in_specs=(P(ROWS, None), P(ROWS, None), P(None, VOCAB), P(None, VOCAB_ROWS), P(ROWS)),
        out_specs=(P(ROWS, None), P(ROWS, VOCAB), P(ROWS)),
        check_vma=False,
    )
```

```python
import jax
import jax.numpy as jnp
from jax import lax
from jax.sharding import Mesh
from jax.sharding import PartitionSpec as P


ROWS = ("x", "core")
VOCAB = ("z", "y")
VOCAB_ROWS = ("z", "y", "x", "core")


def shifted(x, axis, by):
    n = lax.axis_size(axis)
    return lax.ppermute(x, axis, [(i, (i + by) % n) for i in range(n)])


def dot(a, b, contract):
    return lax.dot_general(a, b, (contract, ((), ())), preferred_element_type=jnp.float32)


def exchanged(pieces, axis):
    return lax.all_to_all(pieces, axis, 0, 0, tiled=True)


def sent_to_all(x, axis):
    return exchanged(jnp.broadcast_to(x[None], (lax.axis_size(axis), *x.shape)), axis)


def combined(pieces):
    draft_top = jnp.max(pieces[:, 0], axis=0)
    teach_top = jnp.max(pieces[:, 2], axis=0)
    draft_scale = jnp.exp(pieces[:, 0] - draft_top)
    teach_scale = jnp.exp(pieces[:, 2] - teach_top)
    return jnp.stack(
        [
            draft_top,
            jnp.sum(pieces[:, 1] * draft_scale, axis=0),
            teach_top,
            jnp.sum(pieces[:, 3] * teach_scale, axis=0),
            jnp.sum(pieces[:, 4] * teach_scale, axis=0),
        ]
    )


def turned(piece, axis, way):
    ring = lax.axis_size(axis)
    axes = (axis, "core") if axis == "x" else ("core", axis)

    def at(i, c):
        return 2 * (i % ring) + c if axis == "x" else ring * c + i % ring

    pairs = [(at(i, c), at(i + (way, -way)[c], c)) for i in range(ring) for c in range(2)]
    return lax.ppermute(piece, axes, pairs)


def teacher_product(hidden, own):
    place, core = lax.axis_index("x"), lax.axis_index("core")
    ring = lax.axis_size("x")
    half = own.shape[0] // 2

    def product(hidden, mine, others):
        pair = jnp.where(
            core == 0,
            jnp.concatenate([mine, others], axis=1),
            jnp.concatenate([others, mine], axis=1),
        )
        return dot(hidden, pair, ((1,), (0,)))

    behind, ahead = turned(own, "x", 1), turned(own, "x", -1)
    far_top = turned(behind[:half], "x", 1)
    far_low = turned(behind[half:], "x", 1)
    own_part = product(hidden, own, shifted(own, "core", 1))
    behind_part = product(hidden, behind, shifted(ahead, "core", 1))
    ahead_part = product(hidden, ahead, shifted(behind, "core", 1))
    far_part = product(hidden[:, :half], far_top, shifted(far_top, "core", 1))
    far_part = far_part + product(hidden[:, half:], far_low, shifted(far_low, "core", 1))
    width = 2 * own.shape[1]
    back = jnp.where(core == 0, ring - 1, 1)
    logits = jnp.zeros((hidden.shape[0], ring * width), jnp.float32)
    for step, part in ((0, own_part), (back, behind_part), (ring - back, ahead_part), (2, far_part)):
        at = (place + step) % ring
        logits = lax.dynamic_update_slice(logits, part, (0, at * width))
    return logits


def swapped(pieces, axis):
    n, place = lax.axis_size(axis), lax.axis_index(axis)
    found = []
    for by in range(n):
        piece = lax.dynamic_index_in_dim(pieces, (place + by) % n, 0, keepdims=False)
        found.append(shifted(piece, axis, by) if by else piece)
    return found


def gathered(block, axis):
    n, place, core = lax.axis_size(axis), lax.axis_index(axis), lax.axis_index("core")
    back = jnp.where(core == 0, n - 1, 1)
    behind, ahead = turned(block, axis, 1), turned(block, axis, -1)
    far = turned(behind, axis, 1)
    whole = jnp.zeros((n, *block.shape), block.dtype)
    for step, piece in ((0, block), (back, behind), (n - back, ahead), (2, far)):
        whole = lax.dynamic_update_index_in_dim(whole, piece, (place + step) % n, 0)
    return whole


def added(pieces):
    return sum(piece.astype(jnp.float32) for piece in pieces).astype(jnp.bfloat16)


def summed_head(draft_hidden, grad_logits):
    core = lax.axis_index("core")
    tokens, width = draft_hidden.shape
    ring = lax.axis_size("x")
    strips = draft_hidden.reshape(tokens, ring, 2, width // (2 * ring))

    def strip(which):
        return lax.dynamic_index_in_dim(strips, which, 2, keepdims=False).reshape(tokens, width // 2)

    away = dot(strip(1 - core), grad_logits, ((0,), (0,))).astype(jnp.bfloat16)
    away = shifted(away, "core", 1)
    mine = dot(strip(core), grad_logits, ((0,), (0,)))
    pair = (mine + away.astype(jnp.float32)).astype(jnp.bfloat16)
    pieces = swapped(pair.reshape(ring, -1, pair.shape[1]), "x")
    return added(pieces)


def summed(part):
    n, m = lax.axis_size("y"), lax.axis_size("z")
    pieces = swapped(part.reshape(n, -1, part.shape[1]), "y")
    rows = added(pieces)
    pieces = exchanged(rows.reshape(m, -1, rows.shape[1]), "z")
    block = added(pieces)
    rows = sent_to_all(block, "z").reshape(rows.shape)
    return gathered(rows, "y").reshape(part.shape)


def stage(draft_hidden, teacher_hidden, draft_head, teacher_head, row_weight):
    draft_logits = dot(draft_hidden, draft_head, ((1,), (0,)))
    local_draft = jnp.max(draft_logits, axis=1)
    teacher_logits = teacher_product(teacher_hidden, teacher_head)
    local_teach = jnp.max(teacher_logits, axis=1)
    teach_exp = jnp.exp(teacher_logits - local_teach[:, None])
    stats = jnp.stack(
        [
            local_draft,
            jnp.sum(jnp.exp(draft_logits - local_draft[:, None]), axis=1),
            local_teach,
            jnp.sum(teach_exp, axis=1),
            jnp.sum(teach_exp * (teacher_logits - draft_logits), axis=1),
        ]
    )
    stats = combined(sent_to_all(stats, "y"))
    draft_top, draft_sum, teach_top, teach_sum, teach_gap = combined(sent_to_all(stats, "z"))
    draft_lse = draft_top + jnp.log(draft_sum)
    teacher_lse = teach_top + jnp.log(teach_sum)
    kl_rows = row_weight * (teach_gap / teach_sum - teacher_lse + draft_lse)
    teacher_prob = jnp.exp(teacher_logits - teacher_lse[:, None])
    draft_prob = jnp.exp(draft_logits - draft_lse[:, None])
    grad_logits = (row_weight[:, None] * (draft_prob - teacher_prob)).astype(jnp.bfloat16)
    grad_head = summed_head(draft_hidden, grad_logits)
    hidden_part = dot(grad_logits, draft_head, ((1,), (1,))).astype(jnp.bfloat16)
    grad_hidden = summed(hidden_part)
    return (grad_hidden, grad_head, kl_rows)


def solution(mesh):
    finer = Mesh(mesh.devices.reshape(4, 2, 8, 4), ("x", "core", "z", "y"))
    return jax.shard_map(
        stage,
        mesh=finer,
        in_specs=(P(ROWS, None), P(ROWS, None), P(None, VOCAB), P(None, VOCAB_ROWS), P(ROWS)),
        out_specs=(P(ROWS, None), P(ROWS, VOCAB), P(ROWS)),
        check_vma=False,
    )
```

```python
import jax
import jax.numpy as jnp
from jax import lax
from jax.sharding import Mesh
from jax.sharding import PartitionSpec as P


ROWS = ("x", "core")
VOCAB = ("z", "y")
VOCAB_ROWS = ("z", "y", "x", "core")


def shifted(x, axis, by):
    n = lax.axis_size(axis)
    return lax.ppermute(x, axis, [(i, (i + by) % n) for i in range(n)])


def dot(a, b, contract):
    return lax.dot_general(a, b, (contract, ((), ())), preferred_element_type=jnp.float32)


def exchanged(pieces, axis):
    return lax.all_to_all(pieces, axis, 0, 0, tiled=True)


def sent_to_all(x, axis):
    return exchanged(jnp.broadcast_to(x[None], (lax.axis_size(axis), *x.shape)), axis)


def combined(pieces):
    draft_top = jnp.max(pieces[:, 0], axis=0)
    teach_top = jnp.max(pieces[:, 2], axis=0)
    draft_scale = jnp.exp(pieces[:, 0] - draft_top)
    teach_scale = jnp.exp(pieces[:, 2] - teach_top)
    return jnp.stack(
        [
            draft_top,
            jnp.sum(pieces[:, 1] * draft_scale, axis=0),
            teach_top,
            jnp.sum(pieces[:, 3] * teach_scale, axis=0),
            jnp.sum(pieces[:, 4] * teach_scale, axis=0),
        ]
    )


def turned(piece, axis, way):
    ring = lax.axis_size(axis)
    axes = (axis, "core") if axis == "x" else ("core", axis)

    def at(i, c):
        return 2 * (i % ring) + c if axis == "x" else ring * c + i % ring

    pairs = [(at(i, c), at(i + (way, -way)[c], c)) for i in range(ring) for c in range(2)]
    return lax.ppermute(piece, axes, pairs)


def teacher_product(hidden, own):
    place, core = lax.axis_index("x"), lax.axis_index("core")
    ring = lax.axis_size("x")
    half = own.shape[0] // 2

    def in_order(mine, others):
        return jnp.where(
            core == 0,
            jnp.concatenate([mine, others], axis=1),
            jnp.concatenate([others, mine], axis=1),
        )

    def product(hidden, *pieces):
        return dot(hidden, in_order(*pieces), ((1,), (0,)))

    behind, ahead = turned(own, "x", 1), turned(own, "x", -1)
    far_top = turned(behind[:half], "x", 1)
    far_low = turned(behind[half:], "x", 1)
    own_part = product(hidden, own, shifted(own, "core", 1))
    behind_too, ahead_too = shifted(behind, "core", 1), shifted(ahead, "core", 1)
    near = jnp.where(
        core == 0,
        jnp.concatenate([behind, ahead_too, ahead, behind_too], axis=1),
        jnp.concatenate([ahead_too, behind, behind_too, ahead], axis=1),
    )
    near_part = dot(hidden, near, ((1,), (0,)))
    far_part = product(hidden[:, :half], far_top, shifted(far_top, "core", 1))
    far_part = product(hidden[:, half:], far_low, shifted(far_low, "core", 1)) + far_part
    width = 2 * own.shape[1]
    back = jnp.where(core == 0, ring - 1, 1)
    logits = jnp.zeros((hidden.shape[0], ring * width), jnp.float32)
    for step, part in ((0, own_part), (back, near_part[:, :width]), (ring - back, near_part[:, width:]), (2, far_part)):
        at = (place + step) % ring
        logits = lax.dynamic_update_slice(logits, part, (0, at * width))
    return logits


def swapped(pieces, axis):
    n, place = lax.axis_size(axis), lax.axis_index(axis)
    found = []
    for by in range(n):
        piece = lax.dynamic_index_in_dim(pieces, (place + by) % n, 0, keepdims=False)
        found.append(shifted(piece, axis, by) if by else piece)
    return found


def gathered(block, axis):
    n, place, core = lax.axis_size(axis), lax.axis_index(axis), lax.axis_index("core")
    back = jnp.where(core == 0, n - 1, 1)
    behind, ahead = turned(block, axis, 1), turned(block, axis, -1)
    far = turned(behind, axis, 1)
    whole = jnp.zeros((n, *block.shape), block.dtype)
    for step, piece in ((0, block), (back, behind), (n - back, ahead), (2, far)):
        whole = lax.dynamic_update_index_in_dim(whole, piece, (place + step) % n, 0)
    return whole


def added(pieces):
    return sum(piece.astype(jnp.float32) for piece in pieces).astype(jnp.bfloat16)


def summed_head(draft_hidden, grad_logits):
    core = lax.axis_index("core")
    width = draft_hidden.shape[1]
    ring = lax.axis_size("x")
    block = width // (2 * ring)

    def strip(which):
        starts = [(2 * i + which) * block for i in range(ring)]
        pieces = [lax.dynamic_slice_in_dim(draft_hidden, at, block, 1) for at in starts]
        return jnp.concatenate(pieces, axis=1)

    away = dot(strip(1 - core), grad_logits, ((0,), (0,))).astype(jnp.bfloat16)
    away = shifted(away, "core", 1)
    mine = dot(strip(core), grad_logits, ((0,), (0,)))
    pair = (mine + away.astype(jnp.float32)).astype(jnp.bfloat16)
    pieces = swapped(pair.reshape(ring, -1, pair.shape[1]), "x")
    return added(pieces)


def summed(part):
    n, m = lax.axis_size("y"), lax.axis_size("z")
    pieces = swapped(part.reshape(n, -1, part.shape[1]), "y")
    rows = added(pieces)
    pieces = exchanged(rows.reshape(m, -1, rows.shape[1]), "z")
    block = added(pieces)
    rows = sent_to_all(block, "z").reshape(rows.shape)
    return gathered(rows, "y").reshape(part.shape)


def stage(draft_hidden, teacher_hidden, draft_head, teacher_head, row_weight):
    draft_logits = dot(draft_hidden, draft_head, ((1,), (0,)))
    local_draft = jnp.max(draft_logits, axis=1)
    teacher_logits = teacher_product(teacher_hidden, teacher_head)
    local_teach = jnp.max(teacher_logits, axis=1)
    teach_exp = jnp.exp(teacher_logits - local_teach[:, None])
    stats = jnp.stack(
        [
            local_draft,
            jnp.sum(jnp.exp(draft_logits - local_draft[:, None]), axis=1),
            local_teach,
            jnp.sum(teach_exp, axis=1),
            jnp.sum(teach_exp * (teacher_logits - draft_logits), axis=1),
        ]
    )
    stats = combined(sent_to_all(stats, "y"))
    draft_top, draft_sum, teach_top, teach_sum, teach_gap = combined(sent_to_all(stats, "z"))
    draft_lse = draft_top + jnp.log(draft_sum)
    teacher_lse = teach_top + jnp.log(teach_sum)
    kl_rows = row_weight * (teach_gap / teach_sum - teacher_lse + draft_lse)
    teacher_prob = jnp.exp(teacher_logits - teacher_lse[:, None])
    draft_prob = jnp.exp(draft_logits - draft_lse[:, None])
    grad_logits = (row_weight[:, None] * (draft_prob - teacher_prob)).astype(jnp.bfloat16)
    grad_head = summed_head(draft_hidden, grad_logits)
    hidden_part = dot(grad_logits, draft_head, ((1,), (1,))).astype(jnp.bfloat16)
    grad_hidden = summed(hidden_part)
    return (grad_hidden, grad_head, kl_rows)


def solution(mesh):
    finer = Mesh(mesh.devices.reshape(4, 2, 8, 4), ("x", "core", "z", "y"))
    return jax.shard_map(
        stage,
        mesh=finer,
        in_specs=(P(ROWS, None), P(ROWS, None), P(None, VOCAB), P(None, VOCAB_ROWS), P(ROWS)),
        out_specs=(P(ROWS, None), P(ROWS, VOCAB), P(ROWS)),
        check_vma=False,
    )
```

```python
import jax
import jax.numpy as jnp
from jax import lax
from jax.sharding import Mesh
from jax.sharding import PartitionSpec as P


ROWS = ("x", "core")
VOCAB = ("z", "y")
VOCAB_ROWS = ("z", "y", "x", "core")


def shifted(x, axis, by):
    n = lax.axis_size(axis)
    return lax.ppermute(x, axis, [(i, (i + by) % n) for i in range(n)])


def dot(a, b, contract):
    return lax.dot_general(a, b, (contract, ((), ())), preferred_element_type=jnp.float32)


def exchanged(pieces, axis):
    return lax.all_to_all(pieces, axis, 0, 0, tiled=True)


def sent_to_all(x, axis):
    return exchanged(jnp.broadcast_to(x[None], (lax.axis_size(axis), *x.shape)), axis)


def combined(pieces):
    draft_top = jnp.max(pieces[:, 0], axis=0)
    teach_top = jnp.max(pieces[:, 2], axis=0)
    draft_scale = jnp.exp(pieces[:, 0] - draft_top)
    teach_scale = jnp.exp(pieces[:, 2] - teach_top)
    return jnp.stack(
        [
            draft_top,
            jnp.sum(pieces[:, 1] * draft_scale, axis=0),
            teach_top,
            jnp.sum(pieces[:, 3] * teach_scale, axis=0),
            jnp.sum(pieces[:, 4] * teach_scale, axis=0),
        ]
    )


def turned(piece, axis, way):
    ring = lax.axis_size(axis)
    axes = (axis, "core") if axis == "x" else ("core", axis)

    def at(i, c):
        return 2 * (i % ring) + c if axis == "x" else ring * c + i % ring

    pairs = [(at(i, c), at(i + (way, -way)[c], c)) for i in range(ring) for c in range(2)]
    return lax.ppermute(piece, axes, pairs)


def teacher_product(hidden, own):
    place, core = lax.axis_index("x"), lax.axis_index("core")
    ring = lax.axis_size("x")
    half = own.shape[0] * 3 // 4

    def in_order(mine, others):
        return jnp.where(
            core == 0,
            jnp.concatenate([mine, others], axis=1),
            jnp.concatenate([others, mine], axis=1),
        )

    def product(hidden, *pieces):
        return dot(hidden, in_order(*pieces), ((1,), (0,)))

    behind, ahead = turned(own, "x", 1), turned(own, "x", -1)
    far_top = turned(behind[:half], "x", 1)
    far_low = turned(behind[half:], "x", 1)
    own_part = product(hidden, own, shifted(own, "core", 1))
    behind_too, ahead_too = shifted(behind, "core", 1), shifted(ahead, "core", 1)
    near = jnp.where(
        core == 0,
        jnp.concatenate([behind, ahead_too, ahead, behind_too], axis=1),
        jnp.concatenate([ahead_too, behind, behind_too, ahead], axis=1),
    )
    near_part = dot(hidden, near, ((1,), (0,)))
    far_part = product(hidden[:, :half], far_top, shifted(far_top, "core", 1))
    far_part = product(hidden[:, half:], far_low, shifted(far_low, "core", 1)) + far_part
    width = 2 * own.shape[1]
    back = jnp.where(core == 0, ring - 1, 1)
    logits = jnp.zeros((hidden.shape[0], ring * width), jnp.float32)
    for step, part in ((0, own_part), (back, near_part[:, :width]), (ring - back, near_part[:, width:]), (2, far_part)):
        at = (place + step) % ring
        logits = lax.dynamic_update_slice(logits, part, (0, at * width))
    return logits


def swapped(pieces, axis):
    n, place = lax.axis_size(axis), lax.axis_index(axis)
    found = []
    for by in range(n):
        piece = lax.dynamic_index_in_dim(pieces, (place + by) % n, 0, keepdims=False)
        found.append(shifted(piece, axis, by) if by else piece)
    return found


def gathered(block, axis):
    n, place, core = lax.axis_size(axis), lax.axis_index(axis), lax.axis_index("core")
    back = jnp.where(core == 0, n - 1, 1)
    behind, ahead = turned(block, axis, 1), turned(block, axis, -1)
    far = turned(behind, axis, 1)
    whole = jnp.zeros((n, *block.shape), block.dtype)
    for step, piece in ((0, block), (back, behind), (n - back, ahead), (2, far)):
        whole = lax.dynamic_update_index_in_dim(whole, piece, (place + step) % n, 0)
    return whole


def added(pieces):
    return sum(piece.astype(jnp.float32) for piece in pieces).astype(jnp.bfloat16)


def summed_head(draft_hidden, grad_logits):
    core = lax.axis_index("core")
    width = draft_hidden.shape[1]
    ring = lax.axis_size("x")
    block = width // (2 * ring)

    def strip(which):
        starts = [(2 * i + which) * block for i in range(ring)]
        pieces = [lax.dynamic_slice_in_dim(draft_hidden, at, block, 1) for at in starts]
        return jnp.concatenate(pieces, axis=1)

    away = dot(strip(1 - core), grad_logits, ((0,), (0,))).astype(jnp.bfloat16)
    away = shifted(away, "core", 1)
    mine = dot(strip(core), grad_logits, ((0,), (0,)))
    pair = (mine + away.astype(jnp.float32)).astype(jnp.bfloat16)
    pieces = swapped(pair.reshape(ring, -1, pair.shape[1]), "x")
    return added(pieces)


def summed_ring(pieces, axis):
    n, place, core = lax.axis_size(axis), lax.axis_index(axis), lax.axis_index("core")
    back = jnp.where(core == 0, n - 1, 1)

    def piece(step):
        return lax.dynamic_index_in_dim(pieces, (place + step) % n, 0, keepdims=False)

    far = turned(piece(2), axis, 1)
    other = turned(piece(back), axis, -1)
    on = turned(added([far, piece(n - back)]), axis, 1)
    return added([piece(0), other, on])


def summed(part):
    n, m = lax.axis_size("y"), lax.axis_size("z")
    rows = summed_ring(part.reshape(n, -1, part.shape[1]), "y")
    pieces = exchanged(rows.reshape(m, -1, rows.shape[1]), "z")
    block = added(pieces)
    rows = sent_to_all(block, "z").reshape(rows.shape)
    return gathered(rows, "y").reshape(part.shape)


def stage(draft_hidden, teacher_hidden, draft_head, teacher_head, row_weight):
    draft_logits = dot(draft_hidden, draft_head, ((1,), (0,)))
    local_draft = jnp.max(draft_logits, axis=1)
    teacher_logits = teacher_product(teacher_hidden, teacher_head)
    local_teach = jnp.max(teacher_logits, axis=1)
    teach_exp = jnp.exp(teacher_logits - local_teach[:, None])
    stats = jnp.stack(
        [
            local_draft,
            jnp.sum(jnp.exp(draft_logits - local_draft[:, None]), axis=1),
            local_teach,
            jnp.sum(teach_exp, axis=1),
            jnp.sum(teach_exp * (teacher_logits - draft_logits), axis=1),
        ]
    )
    stats = combined(sent_to_all(stats, "y"))
    draft_top, draft_sum, teach_top, teach_sum, teach_gap = combined(sent_to_all(stats, "z"))
    draft_lse = draft_top + jnp.log(draft_sum)
    teacher_lse = teach_top + jnp.log(teach_sum)
    kl_rows = row_weight * (teach_gap / teach_sum - teacher_lse + draft_lse)
    teacher_prob = jnp.exp(teacher_logits - teacher_lse[:, None])
    draft_prob = jnp.exp(draft_logits - draft_lse[:, None])
    grad_logits = (row_weight[:, None] * (draft_prob - teacher_prob)).astype(jnp.bfloat16)
    grad_head = summed_head(draft_hidden, grad_logits)
    hidden_part = dot(grad_logits, draft_head, ((1,), (1,))).astype(jnp.bfloat16)
    grad_hidden = summed(hidden_part)
    return (grad_hidden, grad_head, kl_rows)


def solution(mesh):
    finer = Mesh(mesh.devices.reshape(4, 2, 8, 4), ("x", "core", "z", "y"))
    return jax.shard_map(
        stage,
        mesh=finer,
        in_specs=(P(ROWS, None), P(ROWS, None), P(None, VOCAB), P(None, VOCAB_ROWS), P(ROWS)),
        out_specs=(P(ROWS, None), P(ROWS, VOCAB), P(ROWS)),
        check_vma=False,
    )
```

```python
import jax
import jax.numpy as jnp
from jax import lax
from jax.sharding import Mesh
from jax.sharding import PartitionSpec as P


ROWS = ("x", "core")
VOCAB = ("z", "y")
VOCAB_ROWS = ("z", "y", "x", "core")


def shifted(x, axis, by):
    n = lax.axis_size(axis)
    return lax.ppermute(x, axis, [(i, (i + by) % n) for i in range(n)])


def dot(a, b, contract):
    return lax.dot_general(a, b, (contract, ((), ())), preferred_element_type=jnp.float32)


def exchanged(pieces, axis):
    return lax.all_to_all(pieces, axis, 0, 0, tiled=True)


def sent_to_all(x, axis):
    return exchanged(jnp.broadcast_to(x[None], (lax.axis_size(axis), *x.shape)), axis)


def combined(pieces):
    draft_top = jnp.max(pieces[:, 0], axis=0)
    teach_top = jnp.max(pieces[:, 2], axis=0)
    draft_scale = jnp.exp(pieces[:, 0] - draft_top)
    teach_scale = jnp.exp(pieces[:, 2] - teach_top)
    return jnp.stack(
        [
            draft_top,
            jnp.sum(pieces[:, 1] * draft_scale, axis=0),
            teach_top,
            jnp.sum(pieces[:, 3] * teach_scale, axis=0),
            jnp.sum(pieces[:, 4] * teach_scale, axis=0),
        ]
    )


def turned(piece, axis, way):
    ring = lax.axis_size(axis)
    axes = (axis, "core") if axis == "x" else ("core", axis)

    def at(i, c):
        return 2 * (i % ring) + c if axis == "x" else ring * c + i % ring

    pairs = [(at(i, c), at(i + (way, -way)[c], c)) for i in range(ring) for c in range(2)]
    return lax.ppermute(piece, axes, pairs)


def teacher_product(hidden, own):
    place, core = lax.axis_index("x"), lax.axis_index("core")
    ring = lax.axis_size("x")
    half = own.shape[0] * 3 // 4

    def in_order(mine, others):
        return jnp.where(
            core == 0,
            jnp.concatenate([mine, others], axis=1),
            jnp.concatenate([others, mine], axis=1),
        )

    def product(hidden, *pieces):
        return dot(hidden, in_order(*pieces), ((1,), (0,)))

    behind, ahead = turned(own, "x", 1), turned(own, "x", -1)
    far_top = turned(behind[:half], "x", 1)
    far_low = turned(behind[half:], "x", 1)
    own_part = product(hidden, own, shifted(own, "core", 1))
    behind_too, ahead_too = shifted(behind, "core", 1), shifted(ahead, "core", 1)
    near = jnp.where(
        core == 0,
        jnp.concatenate([behind, ahead_too, ahead, behind_too], axis=1),
        jnp.concatenate([ahead_too, behind, behind_too, ahead], axis=1),
    )
    near_part = dot(hidden, near, ((1,), (0,)))
    far_part = product(hidden[:, :half], far_top, shifted(far_top, "core", 1))
    far_part = product(hidden[:, half:], far_low, shifted(far_low, "core", 1)) + far_part
    width = 2 * own.shape[1]
    back = jnp.where(core == 0, ring - 1, 1)
    logits = jnp.zeros((hidden.shape[0], ring * width), jnp.float32)
    for step, part in ((0, own_part), (back, near_part[:, :width]), (ring - back, near_part[:, width:]), (2, far_part)):
        at = (place + step) % ring
        logits = lax.dynamic_update_slice(logits, part, (0, at * width))
    return logits


def swapped(pieces, axis):
    n, place = lax.axis_size(axis), lax.axis_index(axis)
    found = []
    for by in range(n):
        piece = lax.dynamic_index_in_dim(pieces, (place + by) % n, 0, keepdims=False)
        found.append(shifted(piece, axis, by) if by else piece)
    return found


def gathered(block, axis):
    n, place, core = lax.axis_size(axis), lax.axis_index(axis), lax.axis_index("core")
    back = jnp.where(core == 0, n - 1, 1)
    behind, ahead = turned(block, axis, 1), turned(block, axis, -1)
    far = turned(behind, axis, 1)
    whole = jnp.zeros((n, *block.shape), block.dtype)
    for step, piece in ((0, block), (back, behind), (n - back, ahead), (2, far)):
        whole = lax.dynamic_update_index_in_dim(whole, piece, (place + step) % n, 0)
    return whole


def added(pieces):
    return sum(piece.astype(jnp.float32) for piece in pieces).astype(jnp.bfloat16)


def summed_head(draft_hidden, grad_logits):
    core = lax.axis_index("core")
    width = draft_hidden.shape[1]
    ring = lax.axis_size("x")
    block = width // (2 * ring)

    def strip(which):
        starts = [(2 * i + which) * block for i in range(ring)]
        pieces = [lax.dynamic_slice_in_dim(draft_hidden, at, block, 1) for at in starts]
        return jnp.concatenate(pieces, axis=1)

    away = dot(strip(1 - core), grad_logits, ((0,), (0,))).astype(jnp.bfloat16)
    away = shifted(away, "core", 1)
    mine = dot(strip(core), grad_logits, ((0,), (0,)))
    pair = (mine + away.astype(jnp.float32)).astype(jnp.bfloat16)
    pieces = swapped(pair.reshape(ring, -1, pair.shape[1]), "x")
    return added(pieces)


def summed_ring(grad_logits, head, axis):
    n, place, core = lax.axis_size(axis), lax.axis_index(axis), lax.axis_index("core")
    back = jnp.where(core == 0, n - 1, 1)

    def product(rows):
        return dot(rows, head, ((1,), (1,))).astype(jnp.bfloat16)

    def piece(pieces, step):
        pieces = pieces.reshape(n, -1, pieces.shape[1])
        return lax.dynamic_index_in_dim(pieces, (place + step) % n, 0, keepdims=False)

    far = turned(product(piece(grad_logits, 2)), axis, 1)
    pieces = product(grad_logits)
    other = turned(piece(pieces, back), axis, -1)
    on = turned(added([far, piece(pieces, n - back)]), axis, 1)
    return added([piece(pieces, 0), other, on])


def summed_product(grad_logits, head):
    m = lax.axis_size("z")
    rows = summed_ring(grad_logits, head, "y")
    pieces = exchanged(rows.reshape(m, -1, rows.shape[1]), "z")
    block = added(pieces)
    rows = sent_to_all(block, "z").reshape(rows.shape)
    return gathered(rows, "y").reshape(-1, rows.shape[1])


def stage(draft_hidden, teacher_hidden, draft_head, teacher_head, row_weight):
    draft_logits = dot(draft_hidden, draft_head, ((1,), (0,)))
    local_draft = jnp.max(draft_logits, axis=1)
    teacher_logits = teacher_product(teacher_hidden, teacher_head)
    local_teach = jnp.max(teacher_logits, axis=1)
    teach_exp = jnp.exp(teacher_logits - local_teach[:, None])
    stats = jnp.stack(
        [
            local_draft,
            jnp.sum(jnp.exp(draft_logits - local_draft[:, None]), axis=1),
            local_teach,
            jnp.sum(teach_exp, axis=1),
            jnp.sum(teach_exp * (teacher_logits - draft_logits), axis=1),
        ]
    )
    stats = combined(sent_to_all(stats, "y"))
    draft_top, draft_sum, teach_top, teach_sum, teach_gap = combined(sent_to_all(stats, "z"))
    draft_lse = draft_top + jnp.log(draft_sum)
    teacher_lse = teach_top + jnp.log(teach_sum)
    kl_rows = row_weight * (teach_gap / teach_sum - teacher_lse + draft_lse)
    teacher_prob = jnp.exp(teacher_logits - teacher_lse[:, None])
    draft_prob = jnp.exp(draft_logits - draft_lse[:, None])
    grad_logits = (row_weight[:, None] * (draft_prob - teacher_prob)).astype(jnp.bfloat16)
    grad_head = summed_head(draft_hidden, grad_logits)
    grad_hidden = summed_product(grad_logits, draft_head)
    return (grad_hidden, grad_head, kl_rows)


def solution(mesh):
    finer = Mesh(mesh.devices.reshape(4, 2, 8, 4), ("x", "core", "z", "y"))
    return jax.shard_map(
        stage,
        mesh=finer,
        in_specs=(P(ROWS, None), P(ROWS, None), P(None, VOCAB), P(None, VOCAB_ROWS), P(ROWS)),
        out_specs=(P(ROWS, None), P(ROWS, VOCAB), P(ROWS)),
        check_vma=False,
    )
```
